32 devices in a mesh: expert: 16 (over z, y, core), tensor: 2 (over x).
Axes of the slice: x: 2, y: 2, z: 4, core: 2. Of those that a mesh axis runs over, the one named last changes fastest.
Arguments:
- tokens: bfloat16 [4096, 2048], P(('expert', 'tensor')), may hold values from -6 to 6
- assignment: int32 [4096], P(('expert', 'tensor')), may hold values from 0 to 15, as said below
- norm_gain: float32 [2048], replicated, may hold values from 0.25 to 1.75
- centroids: bfloat16 [16, 2048], replicated, may hold values from -0.125 to 0.125
- w_in: bfloat16 [16, 2048, 8192], P('expert', None, 'tensor'), may hold values from -0.125 to 0.125
- w_out: bfloat16 [16, 8192, 2048], P('expert', 'tensor'), may hold values from -0.0625 to 0.0625
Outputs:
- mixed: bfloat16 [4096, 2048], P(('expert', 'tensor'))
The draws below stay inside these ranges and needn't reach their ends.
Inputs may be any that keep to these rules, and one draw needn't show every extreme that they name: `assignment`: in each device's block of 128 consecutive tokens every expert is named exactly 8 times.
All inputs are finite; a program needn't handle non-finite values.
Results may differ from the reference program's by a relative error of at most 0.006.
Values may be sent and summed in bfloat16 or wider, within the bound.
A program may use at most 64 MiB of HBM per device.

```python
import jax
import jax.numpy as jnp
from jax import lax

D = 2048
FF = 8192
TOK_DEV = 128
EXPERTS = 16
TOKENS = 4096
N_TENSOR = 2


def draw_assignment(key, part):
    block_keys = jax.random.split(key, TOKENS // TOK_DEV)

    def shuffled(sub_key):
        return jax.random.permutation(sub_key, TOK_DEV) % EXPERTS
    return jax.vmap(shuffled)(block_keys).reshape(TOKENS).astype(jnp.int32)


def block_scale(stream_key, shape, shards, low, largest):
    level, own = 1.0, jax.random.fold_in(stream_key, 6)
    for position, blocks in shards:
        heights = jnp.exp(jax.random.uniform(jax.random.fold_in(own, position), (blocks,), jnp.float32, low / len(shards), largest / len(shards)))
        level = level * jnp.repeat(heights, shape[position] // blocks).reshape([-1 if axis == position else 1 for axis in range(len(shape))])
    return level


def normal_values(rng, dims, spread, most, cuts=(), kind=jnp.bfloat16):
    loudness = block_scale(rng, dims, cuts, -0.22, 0.18) if cuts else 1.0
    entries = jax.random.normal(rng, dims, jnp.float32) * spread * loudness
    return jnp.minimum(jnp.maximum(entries, -most), most).astype(kind)


def setup_inputs(seed: int = 0) -> dict:
    key_of = jax.random.split(jax.random.key(seed), 7)
    tokens = normal_values(key_of[0], (TOKENS, D), 1.0, 6.0, ((0, 32),))
    assignment = draw_assignment(jax.random.fold_in(key_of[6], 71), 0)
    norm_gain = jnp.clip(1.0 + 0.15 * jax.random.normal(key_of[2], (D,), jnp.float32), 0.25, 1.75)
    centroids = normal_values(key_of[3], (EXPERTS, D), D ** -0.5, 0.125)
    w_in = normal_values(key_of[4], (EXPERTS, D, FF), D ** -0.5, 0.125, ((0, 16), (2, 2)))
    w_out = normal_values(key_of[5], (EXPERTS, FF, D), FF ** -0.5, 0.0625, ((0, 16), (1, 2)))
    return dict(tokens=tokens, assignment=assignment, norm_gain=norm_gain, centroids=centroids, w_in=w_in, w_out=w_out)


def layer_norm(values, gain):
    widened = values.astype(jnp.float32)
    average = lax.optimization_barrier(jnp.mean(widened, axis=1, keepdims=True))
    centred = widened - average
    variance = lax.optimization_barrier(jnp.mean(centred * centred, axis=1, keepdims=True))
    return centred * lax.rsqrt(variance + 1e-05) * gain

def reference(tokens, assignment, norm_gain, centroids, w_in, w_out):
    normed = layer_norm(tokens, norm_gain).astype(jnp.bfloat16)
    logits = jnp.dot(tokens, centroids.T, preferred_element_type=jnp.float32)
    column_ids = jnp.arange(EXPERTS, dtype=jnp.int32)
    picked = lax.optimization_barrier(jnp.sum(jnp.where(assignment[:, None] == column_ids[None, :], logits, 0.0), axis=1))
    gate_value = jax.nn.sigmoid(picked)
    ordering = jnp.argsort(assignment, stable=True).astype(jnp.int32)
    grouped = normed[ordering].reshape(EXPERTS, TOKENS // EXPERTS, D)
    block_width = FF // N_TENSOR

    def expert_ffn(operands):
        expert_rows, w_first, w_second = operands
        hidden = jax.nn.gelu(jnp.dot(expert_rows, w_first, preferred_element_type=jnp.float32), approximate=True).astype(jnp.bfloat16)
        blocked_hidden = hidden.reshape(hidden.shape[0], N_TENSOR, block_width).astype(jnp.float32)
        blocked_weight = w_second.reshape(N_TENSOR, block_width, D).astype(jnp.float32)
        block_sum = jnp.einsum('rbf,bfd->brd', blocked_hidden, blocked_weight).astype(jnp.bfloat16)
        return lax.optimization_barrier(jnp.sum(block_sum.astype(jnp.float32), axis=0)).astype(jnp.bfloat16)
    results = lax.map(expert_ffn, (grouped, w_in, w_out)).reshape(TOKENS, D)
    expert_out = jnp.zeros((TOKENS, D), jnp.bfloat16).at[ordering].set(results)
    mixed = tokens.astype(jnp.float32) + gate_value[:, None] * expert_out.astype(jnp.float32)
    return mixed.astype(jnp.bfloat16)
```

```python
import functools

import jax
import jax.numpy as jnp
from jax import lax
from jax.experimental import pallas as pl
from jax.experimental.pallas import tpu as pltpu
from jax.sharding import PartitionSpec as P

MESH = pl.DeviceIdType.MESH
F32 = jnp.float32
BF16 = jnp.bfloat16
CHUNKS = 8
TILE = 512
LAG = 3


def to_blocks(values, dims):
    return values.reshape(*dims, values.shape[-1]).astype(BF16)


def to_rows(blocks):
    wide = blocks.astype(F32)
    return wide.reshape(-1, wide.shape[-1]).astype(BF16)


def kernel(
    n_exp, n_ten, n_chunk,
    tok_ref, assign_ref, gain_ref, cent_ref, w_in_ref, w_out_ref,
    out_ref,
    w1, w2, send, gath, acc, hid, part, part_in, summed, ret,
    w1_sem, w2_sem, a_send, a_recv, g_send, g_recv, p_send, p_recv, r_send, r_recv,
):
    me = lax.axis_index("expert")
    mt = lax.axis_index("tensor")
    rows, width = tok_ref.shape
    per = rows // n_exp
    dc = width // n_chunk
    hidden = w1.shape[2]
    tile = min(TILE, hidden)

    barrier = pltpu.get_barrier_semaphore()

    @pl.loop(1, n_exp)
    def _(k):
        pl.semaphore_signal(barrier, inc=1, device_id={"expert": lax.rem(me + k, n_exp)}, device_id_type=MESH)

    for k in range(1, n_ten):
        pl.semaphore_signal(barrier, inc=1, device_id={"tensor": lax.rem(mt + k, n_ten)}, device_id_type=MESH)

    def w1_copy(c):
        return pltpu.make_async_copy(w_in_ref.at[0, pl.ds(c * dc, dc)], w1.at[c], w1_sem.at[c])

    def w2_copy(c):
        return pltpu.make_async_copy(w_out_ref.at[0, :, pl.ds(c * dc, dc)], w2.at[c], w2_sem.at[c])

    for c in range(n_chunk):
        w1_copy(c).start()
    for c in range(n_chunk):
        w2_copy(c).start()

    expert_of = assign_ref[...]
    onehot = lax.broadcasted_iota(jnp.int32, (n_exp, rows), 0) == expert_of
    row_id = lax.broadcasted_iota(jnp.int32, (rows, rows), 0)
    col_id = lax.broadcasted_iota(jnp.int32, (rows, rows), 1)
    before = jnp.where(row_id < col_id, 1.0, 0.0).astype(BF16)
    rank = jnp.dot(jnp.where(onehot, 1.0, 0.0).astype(BF16), before, preferred_element_type=F32)
    start = lax.broadcasted_iota(jnp.int32, (n_exp, rows), 0).astype(F32) * float(per)
    slot = jnp.sum(jnp.where(onehot, rank + start, 0.0), axis=0, keepdims=True)
    diagonal = row_id == col_id
    slot_col = jnp.sum(jnp.where(diagonal, slot, 0.0), axis=1, keepdims=True)
    perm = jnp.where(row_id.astype(F32) == slot, 1.0, 0.0).astype(BF16)
    back = jnp.where(col_id.astype(F32) == slot_col, 1.0, 0.0).astype(BF16)

    wide = tok_ref[...].astype(F32)
    average = jnp.mean(wide, axis=1, keepdims=True)
    centred = wide - average
    scale = lax.rsqrt(jnp.mean(centred * centred, axis=1, keepdims=True) + 1e-05)

    pl.semaphore_wait(barrier, n_exp - 1 + n_ten - 1)

    def spread(src, dst, c, sends, recvs, slot_ref):
        @pl.loop(1, n_exp)
        def _(k):
            peer = lax.rem(me + k, n_exp)
            pltpu.make_async_remote_copy(
                src_ref=src.at[c, peer], dst_ref=slot_ref(dst, c, me),
                send_sem=sends.at[c], recv_sem=recvs.at[c],
                device_id={"expert": peer}, device_id_type=MESH,
            ).start()

    def spread_all(src, dst, c, sends, recvs, slots_ref):
        return pltpu.make_async_remote_copy(
            src_ref=src.at[c, pl.ds(0, n_exp - 1)], dst_ref=slots_ref(dst, c),
            send_sem=sends.at[c], recv_sem=recvs.at[c],
            device_id={"expert": lax.rem(me + 1, n_exp)}, device_id_type=MESH,
        )

    gath_slot = lambda ref, c, i: ref.at[c, mt, i]
    gath_slots = lambda ref, c: ref.at[c, mt, pl.ds(0, n_exp - 1)]
    ret_slot = lambda ref, c, i: ref.at[c, i]
    ret_slots = lambda ref, c: ref.at[c, pl.ds(0, n_exp - 1)]

    for c in range(n_chunk):
        cols = slice(c * dc, (c + 1) * dc)
        normed = ((tok_ref[:, cols].astype(F32) - average) * scale * gain_ref[:, cols]).astype(BF16)
        ordered = jnp.dot(perm, normed, preferred_element_type=F32)
        send[c] = to_blocks(ordered, (n_exp, per))
        spread(send, gath, c, a_send, a_recv, gath_slot)
        gath[c, mt, me] = send[c, me]

    logits = lax.dot_general(cent_ref[...], tok_ref[...], (((1,), (1,)), ((), ())), preferred_element_type=F32)
    picked = jnp.sum(jnp.where(onehot, logits, 0.0), axis=0, keepdims=True)
    gate_row = jax.nn.sigmoid(picked)
    gate = jnp.sum(jnp.where(diagonal, gate_row, 0.0), axis=1, keepdims=True)

    def partner_copies(src, dst, c, sends, recvs, own):
        copies = []
        for k in range(1, n_ten):
            other = lax.rem(mt + k, n_ten)
            copies.append(pltpu.make_async_remote_copy(
                src_ref=src.at[c, mt if own else other], dst_ref=dst.at[c, mt],
                send_sem=sends.at[c, k - 1], recv_sem=recvs.at[c, k - 1],
                device_id={"tensor": other}, device_id_type=MESH,
            ))
        return copies

    def first(c):
        w1_copy(c).wait()
        for copy in partner_copies(gath, gath, c, g_send, g_recv, True):
            copy.wait_recv()
        x = to_rows(gath[c])
        last = c == n_chunk - 1

        @pl.loop(0, hidden // tile)
        def _(n):
            at = pl.ds(pl.multiple_of(n * tile, tile), tile)
            got = jnp.dot(x, w1[c, :, at], preferred_element_type=F32)
            if c > 0:
                got = got + acc[:, at]
            if last:
                hid[:, at] = jax.nn.gelu(got, approximate=True).astype(BF16)
            else:
                acc[:, at] = got

    for c in range(n_chunk):
        spread_all(send, gath, c, a_send, a_recv, gath_slots).wait_recv()
        for copy in partner_copies(gath, gath, c, g_send, g_recv, True):
            copy.start()
        if c > 0:
            first(c - 1)
    first(n_chunk - 1)

    def reduce(c):
        for copy in partner_copies(part, part_in, c, p_send, p_recv, False):
            copy.wait_recv()
        total = part[c, mt].astype(F32)
        for k in range(1, n_ten):
            total = total + part_in[c, lax.rem(mt + k, n_ten)].astype(F32)
        summed[c] = total.astype(BF16)
        spread(summed, ret, c, r_send, r_recv, ret_slot)
        ret[c, me] = summed[c, me]

    for c in range(n_chunk):
        w2_copy(c).wait()
        got = jnp.dot(hid[...], w2[c], preferred_element_type=F32)
        part[c] = to_blocks(got, (n_ten, n_exp, per))
        for copy in partner_copies(part, part_in, c, p_send, p_recv, False):
            copy.start()
        if c >= LAG:
            reduce(c - LAG)
    for c in range(n_chunk - LAG, n_chunk):
        reduce(c)

    for c in range(n_chunk):
        cols = slice(c * dc, (c + 1) * dc)
        spread_all(summed, ret, c, r_send, r_recv, ret_slots).wait_recv()
        expert_out = jnp.dot(back, to_rows(ret[c]), preferred_element_type=F32)
        out_ref[:, cols] = (tok_ref[:, cols].astype(F32) + gate * expert_out).astype(BF16)

    for c in range(n_chunk):
        spread_all(send, gath, c, a_send, a_recv, gath_slots).wait_send()
        spread_all(summed, ret, c, r_send, r_recv, ret_slots).wait_send()
        for copy in partner_copies(gath, gath, c, g_send, g_recv, True):
            copy.wait_send()
        for copy in partner_copies(part, part_in, c, p_send, p_recv, False):
            copy.wait_send()


def body(n_exp, n_ten, tokens, assignment, norm_gain, centroids, w_in, w_out):
    rows, width = tokens.shape
    per = rows // n_exp
    hidden = w_in.shape[2]
    n_chunk = CHUNKS
    dc = width // n_chunk
    vmem = pl.BlockSpec(memory_space=pltpu.VMEM)
    hbm = pl.BlockSpec(memory_space=pl.ANY)
    dma = pltpu.SemaphoreType.DMA
    return pl.pallas_call(
        functools.partial(kernel, n_exp, n_ten, n_chunk),
        out_shape=jax.ShapeDtypeStruct(tokens.shape, tokens.dtype),
        in_specs=[vmem, vmem, vmem, vmem, hbm, hbm],
        out_specs=vmem,
        scratch_shapes=[
            pltpu.VMEM((n_chunk, dc, hidden), BF16),
            pltpu.VMEM((n_chunk, hidden, dc), BF16),
            pltpu.VMEM((n_chunk, n_exp, per, dc), BF16),
            pltpu.VMEM((n_chunk, n_ten, n_exp, per, dc), BF16),
            pltpu.VMEM((n_ten * rows, hidden), F32),
            pltpu.VMEM((n_ten * rows, hidden), BF16),
            pltpu.VMEM((n_chunk, n_ten, n_exp, per, dc), BF16),
            pltpu.VMEM((n_chunk, n_ten, n_exp, per, dc), BF16),
            pltpu.VMEM((n_chunk, n_exp, per, dc), BF16),
            pltpu.VMEM((n_chunk, n_exp, per, dc), BF16),
            dma((n_chunk,)), dma((n_chunk,)),
            dma((n_chunk,)), dma((n_chunk,)),
            dma((n_chunk, n_ten - 1)), dma((n_chunk, n_ten - 1)),
            dma((n_chunk, n_ten - 1)), dma((n_chunk, n_ten - 1)),
            dma((n_chunk,)), dma((n_chunk,)),
        ],
        compiler_params=pltpu.CompilerParams(
            collective_id=0, has_side_effects=True, vmem_limit_bytes=64_000_000
        ),
    )(tokens, assignment.reshape(1, rows), norm_gain.reshape(1, width), centroids, w_in, w_out)


def solution(mesh):
    return jax.shard_map(
        functools.partial(body, mesh.shape["expert"], mesh.shape["tensor"]),
        mesh=mesh,
        in_specs=(
            P(("expert", "tensor"), None),
            P(("expert", "tensor")),
            P(),
            P(),
            P("expert", None, "tensor"),
            P("expert", "tensor", None),
        ),
        out_specs=P(("expert", "tensor"), None),
        check_vma=False,
    )
```

```python
import functools

import jax
import jax.numpy as jnp
from jax import lax
from jax.experimental import pallas as pl
from jax.experimental.pallas import tpu as pltpu
from jax.sharding import PartitionSpec as P

MESH = pl.DeviceIdType.MESH
F32 = jnp.float32
BF16 = jnp.bfloat16
CHUNKS = 4
TILE = 512
LAG = 2


def to_blocks(values, dims):
    return values.reshape(*dims, values.shape[-1]).astype(BF16)


def to_rows(blocks):
    wide = blocks.astype(F32)
    return wide.reshape(-1, wide.shape[-1]).astype(BF16)


def kernel(
    n_exp, n_ten, n_chunk,
    tok_ref, assign_ref, gain_ref, cent_ref, w_in_ref, w_out_ref,
    out_ref,
    w1, w2, send, gath, acc, hid, part, part_in, summed, ret,
    w1_sem, w2_sem, a_send, a_recv, g_send, g_recv, p_send, p_recv, r_send, r_recv,
):
    me = lax.axis_index("expert")
    mt = lax.axis_index("tensor")
    rows, width = tok_ref.shape
    per = rows // n_exp
    dc = width // n_chunk
    hidden = w1.shape[2]
    tile = min(TILE, hidden)

    barrier = pltpu.get_barrier_semaphore()

    @pl.loop(1, n_exp)
    def _(k):
        pl.semaphore_signal(barrier, inc=1, device_id={"expert": lax.rem(me + k, n_exp)}, device_id_type=MESH)

    for k in range(1, n_ten):
        pl.semaphore_signal(barrier, inc=1, device_id={"tensor": lax.rem(mt + k, n_ten)}, device_id_type=MESH)

    def w1_copy(c):
        return pltpu.make_async_copy(w_in_ref.at[0, pl.ds(c * dc, dc)], w1.at[c], w1_sem.at[c])

    def w2_copy(c):
        return pltpu.make_async_copy(w_out_ref.at[0, :, pl.ds(c * dc, dc)], w2.at[c], w2_sem.at[c])

    for c in range(n_chunk):
        w1_copy(c).start()
    for c in range(n_chunk):
        w2_copy(c).start()

    expert_of = assign_ref[...]
    onehot = lax.broadcasted_iota(jnp.int32, (n_exp, rows), 0) == expert_of
    row_id = lax.broadcasted_iota(jnp.int32, (rows, rows), 0)
    col_id = lax.broadcasted_iota(jnp.int32, (rows, rows), 1)
    before = jnp.where(row_id < col_id, 1.0, 0.0).astype(BF16)
    rank = jnp.dot(jnp.where(onehot, 1.0, 0.0).astype(BF16), before, preferred_element_type=F32)
    start = lax.broadcasted_iota(jnp.int32, (n_exp, rows), 0).astype(F32) * float(per)
    slot = jnp.sum(jnp.where(onehot, rank + start, 0.0), axis=0, keepdims=True)
    diagonal = row_id == col_id
    slot_col = jnp.sum(jnp.where(diagonal, slot, 0.0), axis=1, keepdims=True)
    perm = jnp.where(row_id.astype(F32) == slot, 1.0, 0.0).astype(BF16)
    back = jnp.where(col_id.astype(F32) == slot_col, 1.0, 0.0).astype(BF16)

    wide = tok_ref[...].astype(F32)
    average = jnp.mean(wide, axis=1, keepdims=True)
    centred = wide - average
    scale = lax.rsqrt(jnp.mean(centred * centred, axis=1, keepdims=True) + 1e-05)

    pl.semaphore_wait(barrier, n_exp - 1 + n_ten - 1)

    def spread(src, dst, c, sends, recvs, slot_ref):
        @pl.loop(1, n_exp)
        def _(k):
            peer = lax.rem(me + k, n_exp)
            pltpu.make_async_remote_copy(
                src_ref=src.at[c, peer], dst_ref=slot_ref(dst, c, me),
                send_sem=sends.at[c], recv_sem=recvs.at[c],
                device_id={"expert": peer}, device_id_type=MESH,
            ).start()

    def spread_all(src, dst, c, sends, recvs, slots_ref):
        return pltpu.make_async_remote_copy(
            src_ref=src.at[c, pl.ds(0, n_exp - 1)], dst_ref=slots_ref(dst, c),
            send_sem=sends.at[c], recv_sem=recvs.at[c],
            device_id={"expert": lax.rem(me + 1, n_exp)}, device_id_type=MESH,
        )

    gath_slot = lambda ref, c, i: ref.at[c, mt, i]
    gath_slots = lambda ref, c: ref.at[c, mt, pl.ds(0, n_exp - 1)]
    ret_slot = lambda ref, c, i: ref.at[c, i]
    ret_slots = lambda ref, c: ref.at[c, pl.ds(0, n_exp - 1)]

    def prepare(c):
        cols = slice(c * dc, (c + 1) * dc)
        normed = ((tok_ref[:, cols].astype(F32) - average) * scale * gain_ref[:, cols]).astype(BF16)
        ordered = jnp.dot(perm, normed, preferred_element_type=F32)
        send[c] = to_blocks(ordered, (n_exp, per))
        spread(send, gath, c, a_send, a_recv, gath_slot)
        gath[c, mt, me] = send[c, me]

    for c in range(2):
        prepare(c)

    logits = lax.dot_general(cent_ref[...], tok_ref[...], (((1,), (1,)), ((), ())), preferred_element_type=F32)
    picked = jnp.sum(jnp.where(onehot, logits, 0.0), axis=0, keepdims=True)
    gate_row = jax.nn.sigmoid(picked)
    gate = jnp.sum(jnp.where(diagonal, gate_row, 0.0), axis=1, keepdims=True)

    def partner_copies(src, dst, c, sends, recvs, own):
        copies = []
        for k in range(1, n_ten):
            other = lax.rem(mt + k, n_ten)
            copies.append(pltpu.make_async_remote_copy(
                src_ref=src.at[c, mt if own else other], dst_ref=dst.at[c, mt],
                send_sem=sends.at[c, k - 1], recv_sem=recvs.at[c, k - 1],
                device_id={"tensor": other}, device_id_type=MESH,
            ))
        return copies

    def first(c):
        w1_copy(c).wait()
        for copy in partner_copies(gath, gath, c, g_send, g_recv, True):
            copy.wait_recv()
        x = to_rows(gath[c])
        last = c == n_chunk - 1

        @pl.loop(0, hidden // tile)
        def _(n):
            at = pl.ds(pl.multiple_of(n * tile, tile), tile)
            got = jnp.dot(x, w1[c, :, at], preferred_element_type=F32)
            if c > 0:
                got = got + acc[:, at]
            if last:
                hid[:, at] = jax.nn.gelu(got, approximate=True).astype(BF16)
            else:
                acc[:, at] = got

    for c in range(n_chunk):
        spread_all(send, gath, c, a_send, a_recv, gath_slots).wait_recv()
        for copy in partner_copies(gath, gath, c, g_send, g_recv, True):
            copy.start()
        if c + 2 < n_chunk:
            prepare(c + 2)
        if c > 0:
            first(c - 1)
    first(n_chunk - 1)

    def reduce(c):
        for copy in partner_copies(part, part_in, c, p_send, p_recv, False):
            copy.wait_recv()
        total = part[c, mt].astype(F32)
        for k in range(1, n_ten):
            total = total + part_in[c, lax.rem(mt + k, n_ten)].astype(F32)
        summed[c] = total.astype(BF16)
        spread(summed, ret, c, r_send, r_recv, ret_slot)
        ret[c, me] = summed[c, me]

    for c in range(n_chunk):
        w2_copy(c).wait()
        got = jnp.dot(hid[...], w2[c], preferred_element_type=F32)
        part[c] = to_blocks(got, (n_ten, n_exp, per))
        for copy in partner_copies(part, part_in, c, p_send, p_recv, False):
            copy.start()
        if c >= LAG:
            reduce(c - LAG)
    for c in range(n_chunk - LAG, n_chunk):
        reduce(c)

    for c in range(n_chunk):
        cols = slice(c * dc, (c + 1) * dc)
        spread_all(summed, ret, c, r_send, r_recv, ret_slots).wait_recv()
        expert_out = jnp.dot(back, to_rows(ret[c]), preferred_element_type=F32)
        out_ref[:, cols] = (tok_ref[:, cols].astype(F32) + gate * expert_out).astype(BF16)

    for c in range(n_chunk):
        spread_all(send, gath, c, a_send, a_recv, gath_slots).wait_send()
        spread_all(summed, ret, c, r_send, r_recv, ret_slots).wait_send()
        for copy in partner_copies(gath, gath, c, g_send, g_recv, True):
            copy.wait_send()
        for copy in partner_copies(part, part_in, c, p_send, p_recv, False):
            copy.wait_send()


def body(n_exp, n_ten, tokens, assignment, norm_gain, centroids, w_in, w_out):
    rows, width = tokens.shape
    per = rows // n_exp
    hidden = w_in.shape[2]
    n_chunk = CHUNKS
    dc = width // n_chunk
    vmem = pl.BlockSpec(memory_space=pltpu.VMEM)
    hbm = pl.BlockSpec(memory_space=pl.ANY)
    dma = pltpu.SemaphoreType.DMA
    return pl.pallas_call(
        functools.partial(kernel, n_exp, n_ten, n_chunk),
        out_shape=jax.ShapeDtypeStruct(tokens.shape, tokens.dtype),
        in_specs=[vmem, vmem, vmem, vmem, hbm, hbm],
        out_specs=vmem,
        scratch_shapes=[
            pltpu.VMEM((n_chunk, dc, hidden), BF16),
            pltpu.VMEM((n_chunk, hidden, dc), BF16),
            pltpu.VMEM((n_chunk, n_exp, per, dc), BF16),
            pltpu.VMEM((n_chunk, n_ten, n_exp, per, dc), BF16),
            pltpu.VMEM((n_ten * rows, hidden), F32),
            pltpu.VMEM((n_ten * rows, hidden), BF16),
            pltpu.VMEM((n_chunk, n_ten, n_exp, per, dc), BF16),
            pltpu.VMEM((n_chunk, n_ten, n_exp, per, dc), BF16),
            pltpu.VMEM((n_chunk, n_exp, per, dc), BF16),
            pltpu.VMEM((n_chunk, n_exp, per, dc), BF16),
            dma((n_chunk,)), dma((n_chunk,)),
            dma((n_chunk,)), dma((n_chunk,)),
            dma((n_chunk, n_ten - 1)), dma((n_chunk, n_ten - 1)),
            dma((n_chunk, n_ten - 1)), dma((n_chunk, n_ten - 1)),
            dma((n_chunk,)), dma((n_chunk,)),
        ],
        compiler_params=pltpu.CompilerParams(
            collective_id=0, has_side_effects=True, vmem_limit_bytes=64_000_000
        ),
    )(tokens, assignment.reshape(1, rows), norm_gain.reshape(1, width), centroids, w_in, w_out)


def solution(mesh):
    return jax.shard_map(
        functools.partial(body, mesh.shape["expert"], mesh.shape["tensor"]),
        mesh=mesh,
        in_specs=(
            P(("expert", "tensor"), None),
            P(("expert", "tensor")),
            P(),
            P(),
            P("expert", None, "tensor"),
            P("expert", "tensor", None),
        ),
        out_specs=P(("expert", "tensor"), None),
        check_vma=False,
    )
```

```python
import functools

import jax
import jax.numpy as jnp
from jax import lax
from jax.experimental import pallas as pl
from jax.experimental.pallas import tpu as pltpu
from jax.sharding import PartitionSpec as P

MESH = pl.DeviceIdType.MESH
F32 = jnp.float32
BF16 = jnp.bfloat16
PARTS = (2, 2, 2, 2)
TILE = 512
LAG = 2


def to_blocks(values, dims):
    return values.reshape(*dims, values.shape[-1]).astype(BF16)


def to_rows(blocks):
    wide = blocks.astype(F32)
    return wide.reshape(-1, wide.shape[-1]).astype(BF16)


def kernel(
    n_exp, n_ten,
    tok_ref, assign_ref, gain_ref, cent_ref, w_in_ref, w_out_ref,
    out_ref,
    w1, w2, send, gath, acc, hid, part, part_in, summed, ret,
    w1_sem, w2_sem, a_send, a_recv, g_send, g_recv, p_send, p_recv, r_send, r_recv,
):
    me = lax.axis_index("expert")
    mt = lax.axis_index("tensor")
    rows, width = tok_ref.shape
    per = rows // n_exp
    n_chunk = len(PARTS)
    unit = width // sum(PARTS)
    hidden = w1.shape[1]
    tile = min(TILE, hidden)

    def span(c):
        return pl.ds(sum(PARTS[:c]) * unit, PARTS[c] * unit)

    barrier = pltpu.get_barrier_semaphore()

    @pl.loop(1, n_exp)
    def _(k):
        pl.semaphore_signal(barrier, inc=1, device_id={"expert": lax.rem(me + k, n_exp)}, device_id_type=MESH)

    for k in range(1, n_ten):
        pl.semaphore_signal(barrier, inc=1, device_id={"tensor": lax.rem(mt + k, n_ten)}, device_id_type=MESH)

    def w1_copy(c):
        return pltpu.make_async_copy(w_in_ref.at[0, span(c)], w1.at[span(c)], w1_sem.at[c])

    def w2_copy(c):
        return pltpu.make_async_copy(w_out_ref.at[0, :, span(c)], w2.at[:, span(c)], w2_sem.at[c])

    for c in range(n_chunk):
        w1_copy(c).start()
    for c in range(n_chunk):
        w2_copy(c).start()

    expert_of = assign_ref[...]
    onehot = lax.broadcasted_iota(jnp.int32, (n_exp, rows), 0) == expert_of
    row_id = lax.broadcasted_iota(jnp.int32, (rows, rows), 0)
    col_id = lax.broadcasted_iota(jnp.int32, (rows, rows), 1)
    before = jnp.where(row_id < col_id, 1.0, 0.0).astype(BF16)
    rank = jnp.dot(jnp.where(onehot, 1.0, 0.0).astype(BF16), before, preferred_element_type=F32)
    start = lax.broadcasted_iota(jnp.int32, (n_exp, rows), 0).astype(F32) * float(per)
    slot = jnp.sum(jnp.where(onehot, rank + start, 0.0), axis=0, keepdims=True)
    diagonal = row_id == col_id
    slot_col = jnp.sum(jnp.where(diagonal, slot, 0.0), axis=1, keepdims=True)
    perm = jnp.where(row_id.astype(F32) == slot, 1.0, 0.0).astype(BF16)
    back = jnp.where(col_id.astype(F32) == slot_col, 1.0, 0.0).astype(BF16)

    wide = tok_ref[...].astype(F32)
    average = jnp.mean(wide, axis=1, keepdims=True)
    centred = wide - average
    scale = lax.rsqrt(jnp.mean(centred * centred, axis=1, keepdims=True) + 1e-05)

    pl.semaphore_wait(barrier, n_exp - 1 + n_ten - 1)

    def spread(src, dst, c, sends, recvs, slot_ref):
        for k in sorted(range(1, n_exp), key=lambda k: abs(2 * k - n_exp)):
            peer = lax.rem(me + k, n_exp)
            pltpu.make_async_remote_copy(
                src_ref=src.at[peer, :, span(c)], dst_ref=slot_ref(dst, c, me),
                send_sem=sends.at[c], recv_sem=recvs.at[c],
                device_id={"expert": peer}, device_id_type=MESH,
            ).start()

    def spread_all(src, dst, c, sends, recvs, slots_ref):
        return pltpu.make_async_remote_copy(
            src_ref=src.at[pl.ds(0, n_exp - 1), :, span(c)], dst_ref=slots_ref(dst, c),
            send_sem=sends.at[c], recv_sem=recvs.at[c],
            device_id={"expert": lax.rem(me + 1, n_exp)}, device_id_type=MESH,
        )

    gath_slot = lambda ref, c, i: ref.at[mt, i, :, span(c)]
    gath_slots = lambda ref, c: ref.at[mt, pl.ds(0, n_exp - 1), :, span(c)]
    ret_slot = lambda ref, c, i: ref.at[i, :, span(c)]
    ret_slots = lambda ref, c: ref.at[pl.ds(0, n_exp - 1), :, span(c)]

    def prepare(c):
        cols = span(c)
        normed = ((tok_ref[:, cols].astype(F32) - average) * scale * gain_ref[:, cols]).astype(BF16)
        ordered = jnp.dot(perm, normed, preferred_element_type=F32)
        send[:, :, cols] = to_blocks(ordered, (n_exp, per))
        spread(send, gath, c, a_send, a_recv, gath_slot)
        gath[mt, me, :, cols] = send[me, :, cols]

    for c in range(2):
        prepare(c)

    logits = lax.dot_general(cent_ref[...], tok_ref[...], (((1,), (1,)), ((), ())), preferred_element_type=F32)
    picked = jnp.sum(jnp.where(onehot, logits, 0.0), axis=0, keepdims=True)
    gate_row = jax.nn.sigmoid(picked)
    gate = jnp.sum(jnp.where(diagonal, gate_row, 0.0), axis=1, keepdims=True)

    def partner_copies(src, dst, c, sends, recvs, own):
        copies = []
        for k in range(1, n_ten):
            other = lax.rem(mt + k, n_ten)
            copies.append(pltpu.make_async_remote_copy(
                src_ref=src.at[mt if own else other, :, :, span(c)], dst_ref=dst.at[mt, :, :, span(c)],
                send_sem=sends.at[c, k - 1], recv_sem=recvs.at[c, k - 1],
                device_id={"tensor": other}, device_id_type=MESH,
            ))
        return copies

    def first(c):
        w1_copy(c).wait()
        for copy in partner_copies(gath, gath, c, g_send, g_recv, True):
            copy.wait_recv()
        x = to_rows(gath[:, :, :, span(c)])
        last = c == n_chunk - 1

        @pl.loop(0, hidden // tile)
        def _(n):
            at = pl.ds(pl.multiple_of(n * tile, tile), tile)
            got = jnp.dot(x, w1[span(c), at], preferred_element_type=F32)
            if c > 0:
                got = got + acc[:, at]
            if last:
                hid[:, at] = jax.nn.gelu(got, approximate=True).astype(BF16)
            else:
                acc[:, at] = got

    for c in range(n_chunk):
        spread_all(send, gath, c, a_send, a_recv, gath_slots).wait_recv()
        for copy in partner_copies(gath, gath, c, g_send, g_recv, True):
            copy.start()
        if c + 2 < n_chunk:
            prepare(c + 2)
        if c > 0:
            first(c - 1)
    first(n_chunk - 1)

    def reduce(c):
        for copy in partner_copies(part, part_in, c, p_send, p_recv, False):
            copy.wait_recv()
        total = part[mt, :, :, span(c)].astype(F32)
        for k in range(1, n_ten):
            total = total + part_in[lax.rem(mt + k, n_ten), :, :, span(c)].astype(F32)
        summed[:, :, span(c)] = total.astype(BF16)
        spread(summed, ret, c, r_send, r_recv, ret_slot)
        ret[me, :, span(c)] = summed[me, :, span(c)]

    for c in range(n_chunk):
        w2_copy(c).wait()
        got = jnp.dot(hid[...], w2[:, span(c)], preferred_element_type=F32)
        part[:, :, :, span(c)] = to_blocks(got, (n_ten, n_exp, per))
        for copy in partner_copies(part, part_in, c, p_send, p_recv, False):
            copy.start()
        if c >= LAG:
            reduce(c - LAG)
    for c in range(n_chunk - LAG, n_chunk):
        reduce(c)

    for c in range(n_chunk):
        cols = span(c)
        spread_all(summed, ret, c, r_send, r_recv, ret_slots).wait_recv()
        expert_out = jnp.dot(back, to_rows(ret[:, :, cols]), preferred_element_type=F32)
        out_ref[:, cols] = (tok_ref[:, cols].astype(F32) + gate * expert_out).astype(BF16)

    for c in range(n_chunk):
        spread_all(send, gath, c, a_send, a_recv, gath_slots).wait_send()
        spread_all(summed, ret, c, r_send, r_recv, ret_slots).wait_send()
        for copy in partner_copies(gath, gath, c, g_send, g_recv, True):
            copy.wait_send()
        for copy in partner_copies(part, part_in, c, p_send, p_recv, False):
            copy.wait_send()


def body(n_exp, n_ten, tokens, assignment, norm_gain, centroids, w_in, w_out):
    rows, width = tokens.shape
    per = rows // n_exp
    hidden = w_in.shape[2]
    n_chunk = len(PARTS)
    vmem = pl.BlockSpec(memory_space=pltpu.VMEM)
    hbm = pl.BlockSpec(memory_space=pl.ANY)
    dma = pltpu.SemaphoreType.DMA
    return pl.pallas_call(
        functools.partial(kernel, n_exp, n_ten),
        out_shape=jax.ShapeDtypeStruct(tokens.shape, tokens.dtype),
        in_specs=[vmem, vmem, vmem, vmem, hbm, hbm],
        out_specs=vmem,
        scratch_shapes=[
            pltpu.VMEM((width, hidden), BF16),
            pltpu.VMEM((hidden, width), BF16),
            pltpu.VMEM((n_exp, per, width), BF16),
            pltpu.VMEM((n_ten, n_exp, per, width), BF16),
            pltpu.VMEM((n_ten * rows, hidden), F32),
            pltpu.VMEM((n_ten * rows, hidden), BF16),
            pltpu.VMEM((n_ten, n_exp, per, width), BF16),
            pltpu.VMEM((n_ten, n_exp, per, width), BF16),
            pltpu.VMEM((n_exp, per, width), BF16),
            pltpu.VMEM((n_exp, per, width), BF16),
            dma((n_chunk,)), dma((n_chunk,)),
            dma((n_chunk,)), dma((n_chunk,)),
            dma((n_chunk, n_ten - 1)), dma((n_chunk, n_ten - 1)),
            dma((n_chunk, n_ten - 1)), dma((n_chunk, n_ten - 1)),
            dma((n_chunk,)), dma((n_chunk,)),
        ],
        compiler_params=pltpu.CompilerParams(
            collective_id=0, has_side_effects=True, vmem_limit_bytes=64_000_000
        ),
    )(tokens, assignment.reshape(1, rows), norm_gain.reshape(1, width), centroids, w_in, w_out)


def solution(mesh):
    return jax.shard_map(
        functools.partial(body, mesh.shape["expert"], mesh.shape["tensor"]),
        mesh=mesh,
        in_specs=(
            P(("expert", "tensor"), None),
            P(("expert", "tensor")),
            P(),
            P(),
            P("expert", None, "tensor"),
            P("expert", "tensor", None),
        ),
        out_specs=P(("expert", "tensor"), None),
        check_vma=False,
    )
```
